32 devices in a mesh: site: 8 (over z, x), band: 4 (over y, core).
Axes of the slice: x: 2, y: 2, z: 4, core: 2. Of those that a mesh axis runs over, the one named last changes fastest.
Arguments:
- fields: bfloat16 [1024, 8, 4096], P('site', None, 'band'), may hold values from -6 to 6
- factor: bfloat16 [1024, 4, 128], P('site'), may hold values from -0.25 to 0.25
- pattern: int32 [8, 3], P('site'), may hold values 0 or 1
- tx_power: float32 [1024], replicated, may hold values from 30 to 49
- site_position: float32 [2, 1024], replicated, may hold values from 0 to 1, as said below
- candidates: int32 [8, 16], P('site'), may hold values from 0 to 1023, as said below
Outputs:
- best_level: float32 [8, 4096], P('site', 'band')
- sinr_level: float32 [8, 4096], P('site', 'band')
- tile_mean: float32 [8], P('site')
The draws below stay inside these ranges and needn't reach their ends.
Inputs may be any that keep to these rules, and one draw needn't show every extreme that they name: `site_position`: tile t covers column t % 8 and row t // 8 of a grid of 8 x (1) tiles over the window. Site s lies in tile s // 128, which is cut into 16 columns by 8 rows of equal cells, each holding exactly one of the tile's sites. The candidates of tile t are its 16 sites in the top row of cells, in order of cell column; they are distinct.
All inputs are finite; a program needn't handle non-finite values. No bound on the sum of `pattern` on one device may be relied on, other than what follows from the above.
Results may differ from the reference program's by a relative error of at most 0.005.
Values may be sent and summed in bfloat16 or wider, within the bound.
No kernel may reach another device: no remote copies, remote signals or barrier semaphores. Data moves between devices by JAX's collectives and lax.ppermute only.
A program may use at most 192 MiB of HBM per device.

```python
import jax
import jax.numpy as jnp
from jax import lax

SITE_DEV = 128
SITES = 1024
TILES = 8
ROWS = 16
COLS = 256
DEPTH = 4
CAND = 16
N_SITE = 8


def cell_of_site(key):
    keys = jax.random.split(jax.random.fold_in(key, 11), TILES)
    return jax.vmap(lambda single: jax.random.permutation(single, SITE_DEV))(keys).astype(jnp.int32)


def draw_candidates(key, part):
    cells = cell_of_site(key)
    occupant = jnp.argsort(cells, axis=1, stable=True).astype(jnp.int32)
    tile_base = (jnp.arange(TILES, dtype=jnp.int32) * SITE_DEV)[:, None]
    return (tile_base + occupant[:, :CAND]).astype(jnp.int32)


def draw_site_position(key, part):
    cells = cell_of_site(key)
    cell_col = (cells % CAND).astype(jnp.float32)
    cell_row = (cells // CAND).astype(jnp.float32)
    rows_per = float(SITE_DEV // CAND)
    tile_index = jnp.arange(TILES, dtype=jnp.int32)[:, None]
    tile_col = (tile_index % 8).astype(jnp.float32)
    tile_row = (tile_index // 8).astype(jnp.float32)
    jitter = jax.random.uniform(jax.random.fold_in(key, 12), (2, TILES, SITE_DEV), jnp.float32)
    pos_x = (tile_col + (cell_col + jitter[0]) / float(CAND)) / 8.0
    pos_y = tile_row + (cell_row + jitter[1]) / rows_per
    both = jnp.stack([pos_x.reshape(SITES), pos_y.reshape(SITES)], axis=0)
    return jnp.clip(both, 0.0, 1.0).astype(jnp.float32)


def place_ends(array, key, low, top_value):
    longest = array.shape.index(max(array.shape))
    spots = []
    for shift in (0, 1):
        where = [jax.random.randint(jax.random.fold_in(key, axis), (), 0, length) for axis, length in enumerate(array.shape)]
        where[longest] = (where[longest] + shift) % array.shape[longest]
        spots.append(tuple(where))
    return array.at[spots[0]].set(low).at[spots[1]].set(top_value)


def shard_levels(key, dims, cuts, least, top_value):
    level, own = 1.0, jax.random.fold_in(key, 6)
    for dim, blocks in cuts:
        heights = jnp.exp(jax.random.uniform(jax.random.fold_in(own, dim), (blocks,), jnp.float32, least / len(cuts), top_value / len(cuts)))
        level = level * jnp.repeat(heights, dims[dim] // blocks).reshape([-1 if axis == dim else 1 for axis in range(len(dims))])
    return level


def gaussian(stream_key, shape, scale, reach, cuts=(), kind=jnp.bfloat16):
    level = shard_levels(stream_key, shape, cuts, -0.22, 0.18) if cuts else 1.0
    result = jax.random.normal(stream_key, shape, jnp.float32) * scale * level
    return jnp.minimum(jnp.maximum(result, -reach), reach).astype(kind)


def setup_inputs(seed: int = 0) -> dict:
    streams_of = jax.random.split(jax.random.key(seed), 7)
    fields = gaussian(streams_of[0], (SITES, TILES, ROWS * COLS), 1.0, 6.0, ((0, 8), (2, 4)))
    factor = gaussian(streams_of[1], (SITES, DEPTH, SITE_DEV), (DEPTH * SITE_DEV) ** -0.5, 0.25, ((0, 8),))
    pattern = place_ends((jax.random.randint(streams_of[2], (N_SITE, DEPTH - 1), 0, 3) < 2).astype(jnp.int32), jax.random.fold_in(streams_of[2], 1), 0, 1)
    tx_power = jnp.clip(jax.random.uniform(streams_of[3], (SITES,), jnp.float32, 30.0, 49.0), 30.0, 49.0)
    site_position = draw_site_position(jax.random.fold_in(streams_of[6], 71), 0)
    candidates = draw_candidates(jax.random.fold_in(streams_of[6], 71), 0)
    return dict(fields=fields, factor=factor, pattern=pattern, tx_power=tx_power, site_position=site_position, candidates=candidates)


spacing = 0.03
ln_tenth = 0.2302585093

def coverage(mixed, tile_number, row_start, row_count, height, tx_power, site_position, cand_row):
    pixel = jnp.arange(row_count * COLS, dtype=jnp.int32)
    row_index = row_start + pixel // COLS
    col_index = pixel % COLS
    pos_x = (tile_number % 8 * COLS + col_index).astype(jnp.float32) * spacing
    pos_y = (tile_number // 8 * COLS + row_index).astype(jnp.float32) * spacing
    site_x = site_position[0] * (8.0 * COLS * spacing)
    site_y = site_position[1] * (height * COLS * spacing)
    dist = jnp.sqrt((site_x[:, None] - pos_x[None, :]) ** 2 + (site_y[:, None] - pos_y[None, :]) ** 2 + spacing * spacing)
    level = tx_power[:, None] - (100.0 + 22.0 * jnp.log10(dist)) + 8.0 * mixed.astype(jnp.float32) + 90.0
    power = jnp.exp(ln_tenth * level)
    cand_power = jnp.take(power, cand_row, axis=0)
    best = lax.optimization_barrier(jnp.max(cand_power, axis=0))
    serving = jnp.take(cand_row, jnp.argmax(cand_power, axis=0).astype(jnp.int32))
    site_ids = jnp.arange(power.shape[0], dtype=jnp.int32)
    interference = lax.optimization_barrier(jnp.sum(jnp.where(site_ids[:, None] == serving[None, :], 0.0, power), axis=0))
    return (jnp.log10(best), jnp.log10(best / interference))

def reference(fields, factor, pattern, tx_power, site_position, candidates):
    nblocks = SITES // SITE_DEV
    pixels = ROWS * COLS
    blocks = fields.reshape(nblocks, SITE_DEV, TILES, pixels)
    lower = jnp.tril(jnp.ones((SITE_DEV, SITE_DEV), jnp.float32))

    def one_tile(tile_number):
        tile_fields = jnp.take(blocks, tile_number, axis=2)
        total = jnp.zeros((nblocks, SITE_DEV, pixels), jnp.float32)
        for offset in range(DEPTH):
            shifted = jnp.concatenate([jnp.zeros((offset, SITE_DEV, pixels), jnp.bfloat16), tile_fields[:nblocks - offset]], axis=0)
            coef = factor[:, offset, :].reshape(nblocks, SITE_DEV, SITE_DEV).astype(jnp.float32)
            if offset == 0:
                coef = coef * lower
            else:
                coef = coef * pattern[:, offset - 1].astype(jnp.float32)[:, None, None]
            total = total + jnp.einsum('nik,nkp->nip', coef, shifted.astype(jnp.float32), precision=lax.Precision.HIGHEST)
        mixed = total.astype(jnp.bfloat16).reshape(SITES, pixels)
        cand_row = jnp.take(candidates, tile_number, axis=0)
        return coverage(mixed, tile_number, 0, ROWS, TILES // 8, tx_power, site_position, cand_row)
    best_level, sinr_level = lax.map(one_tile, jnp.arange(TILES, dtype=jnp.int32))
    tile_mean = lax.optimization_barrier(jnp.mean(sinr_level, axis=1))
    return (best_level, sinr_level, tile_mean)
```

```python
import functools
import math

import jax
import jax.numpy as jnp
from jax import lax
from jax.experimental import pallas as pl
from jax.experimental.pallas import tpu as pltpu
from jax.sharding import PartitionSpec as P


COLS = 256
spacing = 0.03
ln_tenth = 0.2302585093
to_exp2 = ln_tenth * math.log2(math.e)
dist_gain = to_exp2 * 11.0 * math.log10(2.0)
mixed_gain = to_exp2 * 8.0
F32 = jnp.float32
BF16 = jnp.bfloat16
SPARE = 256 << 10
SHARES = 2
HBM = pl.BlockSpec(memory_space=pltpu.HBM)
SMEM = pl.BlockSpec(memory_space=pltpu.SMEM)
VMEM = pl.BlockSpec(memory_space=pltpu.VMEM)


def places():
    return lax.axis_index("site"), lax.axis_index("band")


def grant(*parts):
    size = sum(math.prod(shape) * jnp.dtype(kind).itemsize for shape, kind in parts)
    return pltpu.CompilerParams(vmem_limit_bytes=min(size + (8 << 20), 60 << 20))


def room_for(*parts):
    size = sum(math.prod(shape) * jnp.dtype(kind).itemsize for shape, kind in parts)
    return pltpu.CompilerParams(vmem_limit_bytes=(64 << 20) - size - SPARE)


def split_tiles(fields, factor, pattern, lines):
    block, tiles, pixels = fields.shape
    depth = factor.shape[1]
    chunk = min(block, max(1, 256 // tiles))
    part = block // SHARES
    wide = depth * block
    np_ = 2 * lines

    def kernel(pattern_ref, x_ref, factor_ref, *refs):
        pairs, (coef_out, x_in, factor_in, sems) = refs[:np_], refs[np_:]
        me, band = places()
        copies = [pltpu.make_async_copy(factor_ref.at[pl.ds(band % SHARES * part, part)], factor_in, sems.at[block // chunk])]
        for i in range(block // chunk):
            span = slice(i * chunk, (i + 1) * chunk)
            copies.append(pltpu.make_async_copy(x_ref.at[span], x_in.at[span], sems.at[i]))
        for copy in copies:
            copy.start()
        size = chunk * tiles
        row = lax.broadcasted_iota(jnp.int32, (size, size), 0)
        col = lax.broadcasted_iota(jnp.int32, (size, size), 1)
        slot = row // chunk
        kind, k, j = slot // (2 * lines), slot // 2 % lines, slot % 2
        tile = (2 * (((me // lines) & 1) ^ 1 ^ kind) + j) * lines + ((me % lines) ^ k)
        move = jnp.where(col == row % chunk * tiles + tile, 1.0, 0.0)
        for i in range(block // chunk):
            copies[i + 1].wait()
            for c in range(0, pixels, 256):
                span = slice(c, c + 256)
                x = x_in[i * chunk : (i + 1) * chunk, :, span].astype(F32).reshape(size, 256)
                moved = jnp.dot(move, x, preferred_element_type=F32).astype(BF16)
                for p, pair in enumerate(pairs):
                    for j in range(2):
                        at = (2 * p + j) * chunk
                        pair[j, i * chunk : (i + 1) * chunk, span] = moved[at : at + chunk]
        copies[0].wait()
        row = lax.broadcasted_iota(jnp.int32, (part, block), 0) + band % SHARES * part
        col = lax.broadcasted_iota(jnp.int32, (part, block), 1)
        rows = factor_in[...].astype(F32)
        for d in range(depth):
            keep = col <= row if d == 0 else jnp.full((part, block), pattern_ref[0, d - 1], jnp.int32) != 0
            lane = (depth - 1 - d) * block
            coef_out[:, lane : lane + block] = jnp.where(keep, rows[:, d, :], 0.0).astype(BF16)

    shapes = [((2, block, pixels), BF16)] * np_ + [((part, wide), BF16)]
    scratch = [((block, tiles, pixels), BF16), ((part, depth, block), BF16)]
    out = pl.pallas_call(
        kernel,
        in_specs=[SMEM, HBM, HBM],
        out_specs=[VMEM] * (np_ + 1),
        out_shape=[jax.ShapeDtypeStruct(*shape) for shape in shapes],
        scratch_shapes=[pltpu.VMEM(*one) for one in scratch] + [pltpu.SemaphoreType.DMA((block // chunk + 1,))],
        compiler_params=room_for(*shapes),
        name="split_tiles",
    )(pattern, fields, factor)
    return out[:lines], out[lines:-1], out[-1]


def tile_of(me, lines, j):
    return (2 * (((me // lines) & 1) ^ 1) + j) * lines + me % lines


def column(ref, row, i, block):
    line = ref[pl.ds(row, 1), pl.ds(pl.multiple_of(i * block, block), block)]
    return jnp.broadcast_to(line, (block, block)).T


def geometry(tx_ref, pos_ref, i, block, height):
    xs = column(pos_ref, 0, i, block) * (8.0 * COLS * spacing)
    ys = column(pos_ref, 1, i, block) * (height * COLS * spacing)
    base = to_exp2 * (column(tx_ref, 0, i, block) - 10.0)
    wide = COLS // block
    return jnp.concatenate([xs] * wide, axis=1), ys, jnp.concatenate([base] * wide, axis=1)


def across(xs, tile):
    col = lax.broadcasted_iota(jnp.int32, (1, COLS), 1)
    dx = xs - (tile % 8 * COLS + col).astype(F32) * spacing
    return dx * dx


def reach(dx2, ys, base, tile, row):
    at = jnp.full(ys.shape, tile // 8 * COLS + row, jnp.int32).astype(F32) * spacing
    dy = ys - at
    dy2 = dy * dy + spacing * spacing
    d2 = dx2 + jnp.concatenate([dy2] * (COLS // ys.shape[1]), axis=1)
    return base - dist_gain * jnp.log2(d2)


def rounded(mixed):
    return mixed_gain * mixed.astype(BF16).astype(F32)


def fold(power):
    return jnp.sum(power.reshape(power.shape[0] // 8, 8, power.shape[1]), axis=0)


def pick(cand_ref, j, first_site, pw, top, block):
    pixels = pw.shape[1]
    best = jnp.full((1, pixels), -1.0, F32)
    serving = jnp.zeros((1, pixels), jnp.int32)
    for c in range(cand_ref.shape[1]):
        local = jnp.clip(cand_ref[j, c] - first_site, 0, block - 1)
        power = pw[pl.ds(top + local, 1), :]
        more = power > best
        best = jnp.where(more, power, best)
        serving = jnp.where(more, local, serving)
    rest = []
    for c in range(0, pixels, COLS):
        ids = lax.broadcasted_iota(jnp.int32, (block, COLS), 0)
        mine = pw[pl.ds(top, block), c : c + COLS]
        rest.append(fold(jnp.where(ids == serving[:, c : c + COLS], 0.0, mine)))
    return best, jnp.concatenate(rest, axis=1)


def reach_tables(tx, pos, unit, half, depth, pixels, height):
    n, lines, lead = 2 * half, half // 2, depth - 1
    block = tx.shape[1] // n
    rows = pixels // COLS
    tall = lead * block

    def kernel(tx_ref, pos_ref, unit_ref, table, median, unit_out):
        unit_out[...] = unit_ref[...]
        me, band = places()
        upper = me // half
        low = upper * half
        level = me // lines

        def fill(out, place, i):
            xs, ys, base = geometry(tx_ref, pos_ref, i, block, height)
            for j in range(2):
                tile = tile_of(me, lines, j)
                dx2 = across(xs, tile)
                for r in range(rows):
                    span = slice(r * COLS, (r + 1) * COLS)
                    out[j, pl.ds(place, block), span] = reach(dx2, ys, base, tile, band * rows + r)

        def body(l, carry):
            fill(table, pl.multiple_of(l * block, block), low + l)
            return carry

        lax.fori_loop(upper * lead, half, body, 0)

        @pl.when((level == 1) | (level == 2))
        def _():
            def inner(l, carry):
                fill(median, pl.multiple_of(l * block, block), half + l)
                return carry

            lax.fori_loop(0, lead, inner, 0)

    outs = [((2, half * block, pixels), F32), ((2, tall, pixels), F32), (unit.shape, BF16)]
    flops = 20 * 2 * (half + lead) * block * pixels
    return pl.pallas_call(
        kernel,
        in_specs=[VMEM] * 3,
        out_specs=[VMEM] * 3,
        out_shape=[jax.ShapeDtypeStruct(*out) for out in outs],
        compiler_params=grant(*outs, outs[2]),
        cost_estimate=pl.CostEstimate(flops=flops, bytes_accessed=8 << 20, transcendentals=0),
        name="reach_tables",
    )(tx, pos, unit)


def stage_one(cand, table, pieces, held, partner, half, depth):
    _, block, pixels = held[0].shape
    lead, lines = depth - 1, half // 2
    rows = pixels // COLS
    n, part, wide = 2 * half, pieces[0].shape[3], depth * block
    np_, nh = len(pieces), len(held)
    tall = lead * block

    def kernel(cand_ref, table_ref, *refs):
        piece_refs, refs = refs[:np_], refs[np_:]
        held_refs, refs = refs[:nh], refs[nh:]
        partner_refs, refs = refs[:nh], refs[nh:]
        sums, best_out, partial, coef_cross = refs[:4]
        near, coef, coef_own, group, pw, acc = refs[4:]
        me, band = places()
        upper = me // half
        low = upper * half
        level = me // lines
        inner = (level == 1) | (level == 2)
        views = [piece.at[m] for piece in piece_refs for m in range(piece.shape[0])]
        for m, view in enumerate(views):
            start = pl.multiple_of((band % SHARES ^ m) * part, part)
            for e in range(n):
                coef[me ^ e, pl.ds(start, part), :] = view[e // lines, e % lines]
        near[:, :lead] = jnp.zeros((2, lead, block, pixels), BF16)
        for k in range(lines):
            for j in range(2):
                near[j, lead + (me ^ k) - low] = held_refs[k][j]
                near[j, lead + (me ^ k ^ lines) - low] = partner_refs[k][j]
        acc[...] = jnp.zeros_like(acc)
        best_out[...] = jnp.zeros_like(best_out)

        @pl.when(inner)
        def _():
            up = jnp.full((block, block), upper, jnp.int32) != 0
            for l in range(lead):
                for c in range(lead):
                    zero = jnp.zeros((block, block), BF16)
                    early = coef[half + l, :, (c - l) * block : (c - l + 1) * block] if c >= l else zero
                    at = lead - l + c
                    late = coef[half + l, :, at * block : (at + 1) * block] if c <= l else zero
                    there = (slice(l * block, (l + 1) * block), slice(c * block, (c + 1) * block))
                    early, late = early.astype(F32), late.astype(F32)
                    coef_own[there] = jnp.where(up, late, early).astype(BF16)
                    coef_cross[there] = jnp.where(up, early, late).astype(BF16)
            top = jnp.where(upper == 0, half, lead)
            for j in range(2):
                for r in range(rows):
                    span = slice(r * COLS, (r + 1) * COLS)
                    some = near[j, pl.ds(top, lead), :, span].reshape(tall, COLS)
                    partial[j, :, span] = jnp.dot(coef_own[...], some, preferred_element_type=F32)

        first = upper * lead

        def add(j, i, span, power):
            own = i == tile_of(me, lines, j)

            @pl.when(own)
            def _():
                pw[j, :, span] = power

            acc[j, :, span] += jnp.where(own, 0.0, fold(power))

        @pl.when(upper == 0)
        def _():
            for g in range(0, half, depth):
                count = min(depth, half - g)
                start = max(0, g - lead)
                deep = g + count - start
                for a in range(count):
                    for b in range(deep):
                        d = g + a - start - b
                        there = (slice(a * block, (a + 1) * block), slice(b * block, (b + 1) * block))
                        if 0 <= d < depth:
                            group[there] = coef[g + a, :, (lead - d) * block : (depth - d) * block]
                        else:
                            group[there] = jnp.zeros((block, block), BF16)
                for j in range(2):
                    for r in range(rows):
                        span = slice(r * COLS, (r + 1) * COLS)
                        some = near[j, lead + start : lead + start + deep, :, span].reshape(deep * block, COLS)
                        here = slice(g * block, (g + count) * block)
                        mixed = jnp.dot(group[: count * block, : deep * block], some, preferred_element_type=F32)
                        power = jnp.exp2(table_ref[j, here, span] + rounded(mixed))
                        for a in range(count):
                            add(j, g + a, span, power[a * block : (a + 1) * block])

        @pl.when(upper != 0)
        def _():
            def body(l, carry):
                for j in range(2):
                    for r in range(rows):
                        span = slice(r * COLS, (r + 1) * COLS)
                        some = near[j, pl.ds(l, depth), :, span].reshape(depth * block, COLS)
                        mixed = rounded(jnp.dot(coef[half + l], some, preferred_element_type=F32))
                        here = pl.ds(pl.multiple_of(l * block, block), block)
                        add(j, half + l, span, jnp.exp2(table_ref[j, here, span] + mixed))
                return carry

            lax.fori_loop(lead, half, body, 0)

        for j in range(2):
            tile = tile_of(me, lines, j)

            @pl.when((tile >= low + first) & (tile < low + half))
            def _():
                best, rest = pick(cand_ref, j, tile * block, pw.at[j], 0, block)
                best_out[j : j + 1] = best
                acc[j] += rest

            sums[j : j + 1] = jnp.sum(acc[j], axis=0, keepdims=True)

    flops = (half * 2 + lead) * 2 * block * depth * block * pixels
    scratch = [
        ((2, lead + half, block, pixels), BF16),
        ((n, block, wide), BF16),
        ((tall, tall), BF16),
        ((depth * block, (depth + lead) * block), BF16),
        ((2, block, pixels), F32),
        ((2, 8, pixels), F32),
    ]
    outs = [((2, pixels), F32)] * 2 + [((2, tall, pixels), F32), ((tall, tall), BF16)]
    given = (table, *pieces, *held, *partner)
    return pl.pallas_call(
        kernel,
        in_specs=[SMEM] + [VMEM] * len(given),
        out_specs=[VMEM] * 4,
        out_shape=[jax.ShapeDtypeStruct(*out) for out in outs],
        scratch_shapes=[pltpu.VMEM(*one) for one in scratch],
        compiler_params=grant(*scratch, *outs, *[(x.shape, x.dtype) for x in given]),
        cost_estimate=pl.CostEstimate(flops=flops, bytes_accessed=8 << 20, transcendentals=0),
        name="stage_one",
    )(cand, *given)


def stage_two(cand, one, median, units, half, depth):
    _, block, pixels = units[0][1].shape
    lead, lines = depth - 1, half // 2
    rows = pixels // COLS
    nu = len(units)
    tall = lead * block

    def kernel(cand_ref, sums, best_one, partial, coef, median, *refs):
        unit_refs, refs = refs[:nu], refs[nu:]
        own_out, hop_out, far, pw, acc, best = refs
        me, _ = places()
        upper = me // half
        level = me // lines

        @pl.when((level == 1) | (level == 2))
        def _():
            for (e, _), ref in zip(units, unit_refs):
                place = (me ^ e) - jnp.where(upper == 0, half, half - lead)
                place = jnp.where((place >= 0) & (place < lead), place, lead)
                for j in range(2):
                    far[j, place] = ref[j]
            best[...] = best_one[...]
            for j in range(2):
                tile = tile_of(me, lines, j)
                for r in range(rows):
                    span = slice(r * COLS, (r + 1) * COLS)
                    some = far[j, :lead, :, span].reshape(tall, COLS)
                    mixed = jnp.dot(coef[...], some, preferred_element_type=F32) + partial[j, :, span]
                    power = jnp.exp2(median[j, :, span] + rounded(mixed))
                    total = jnp.zeros((8, COLS), F32)
                    for l in range(lead):
                        total += jnp.where(tile == half + l, 0.0, fold(power[l * block : (l + 1) * block]))
                    acc[:, span] = total

                    @pl.when(upper != 0)
                    def _():
                        pw[:, span] = power

                @pl.when((tile >= half) & (tile < half + lead))
                def _():
                    top = pl.multiple_of((tile - half) * block, block)
                    first, rest = pick(cand_ref, j, tile * block, pw, top, block)
                    best[j : j + 1] = first
                    acc[...] += rest

                total = sums[j : j + 1] + jnp.sum(acc[...], axis=0, keepdims=True)
                mine = (level == 1) == (j == 1)

                def put(out):
                    out[0:1] = best[j : j + 1]
                    out[1:2] = total

                pl.when(mine)(functools.partial(put, own_out))
                pl.when(jnp.logical_not(mine))(functools.partial(put, hop_out))

    scratch = [((2, lead + 1, block, pixels), BF16), ((tall, pixels), F32), ((8, pixels), F32), ((2, pixels), F32)]
    outs = [jax.ShapeDtypeStruct((2, pixels), F32)] * 2
    given = [x for _, x in units]
    held = [(x.shape, x.dtype) for x in (*one[2:], median, *given)]
    return pl.pallas_call(
        kernel,
        in_specs=[SMEM] + [VMEM] * (5 + nu),
        out_specs=[VMEM] * 2,
        out_shape=outs,
        scratch_shapes=[pltpu.VMEM(*shape) for shape in scratch],
        compiler_params=grant(*scratch, *held),
        name="stage_two",
    )(cand, *one, median, *given)


def finish(own, moved, sums, lines, bands):
    pixels = own.shape[1]

    def kernel(own_ref, moved_ref, inner_ref, ends_ref, best_out, sinr_out, part_out):
        me, _ = places()
        level = me // lines
        inner = (level == 1) | (level == 2)
        at = jnp.where(level < 2, level, level - 2)
        here = jnp.full((1, pixels), jnp.where(inner, 1, 0), jnp.int32) != 0
        best = jnp.where(here, own_ref[0:1], moved_ref[0:1])
        other = jnp.where(here, inner_ref[pl.ds(at, 1)], ends_ref[pl.ds(at, 1)])
        total = jnp.where(here, own_ref[1:2], moved_ref[1:2]) + other
        scale = 1.0 / math.log(10.0)
        sinr = jnp.log(best / total) * scale
        best_out[...] = jnp.log(best) * scale
        sinr_out[...] = sinr
        mean = jnp.sum(sinr, axis=1, keepdims=True) / float(pixels * bands)
        part_out[...] = jnp.broadcast_to(mean, part_out.shape)

    shapes = [(1, pixels), (1, pixels), (1, 128)]
    return pl.pallas_call(
        kernel,
        in_specs=[VMEM] * 4,
        out_specs=[VMEM] * 3,
        out_shape=[jax.ShapeDtypeStruct(shape, F32) for shape in shapes],
        compiler_params=grant(*[(shape, F32) for shape in shapes]),
        name="finish",
    )(own, moved, *sums)


def plan_of(n, lead):
    half, lines = n // 2, n // 4
    row = lambda s, k: s // lines * lines + (s % lines ^ k)
    cross = lambda s, k: half - lead <= row(s, k) < half + lead
    middle = {k: [s for s in range(n) if s // lines in (1, 2) and cross(s, k)] for k in range(lines)}
    outer = {k: [s for s in range(n) if s // lines in (0, 3) and cross(s, k)] for k in range(lines)}
    return middle, outer


def shards(fields, factor, pattern, tx_power, site_position, candidates):
    _, tiles, pixels = fields.shape
    depth = factor.shape[1]
    n, bands = lax.axis_size("site"), lax.axis_size("band")
    half, lines, lead = n // 2, n // 4, depth - 1
    assert tiles == n and half >= lead
    height = tiles // 8
    middle, outer = plan_of(n, lead)
    level = lax.axis_index("site") // lines

    def swap(x, k, axis="site", sources=None):
        count = n if axis == "site" else bands
        sources = range(count) if sources is None else sources
        return lax.ppermute(x, axis, [(s, s ^ k) for s in sources])

    class0, class1, own_part = split_tiles(fields, factor, pattern, lines)

    pass_on = {0: class1[0]}
    pass_on.update({k: swap(class1[k], k) for k in range(1, lines)})
    held = {0: class0[0]}
    held.update({k: swap(class0[k], k) for k in range(1, lines)})
    far = [(3 * lines ^ k, swap(pass_on[k], 3 * lines, sources=middle[k])) for k in range(lines) if middle[k]]
    partner = [swap(pass_on[k], lines) for k in range(lines)]
    far += [(2 * lines ^ k, swap(held[k], 2 * lines, sources=outer[k])) for k in range(lines) if outer[k]]

    line_part = jnp.stack([own_part] + [swap(own_part, k) for k in range(1, lines)])
    senders = [None, range(2 * lines, 3 * lines), range(3 * lines, n)]
    order = [1, 3, 2]
    level_parts = {e: swap(line_part, e * lines, sources=some) for e, some in zip(order, senders)}
    mine = jnp.stack([line_part] + [level_parts[e] for e in range(1, 4)])[None]
    pieces = [mine, swap(mine, 1, axis="band")]

    near_cand = swap(candidates, lines)
    cand = jnp.where(level % 2 == 1, jnp.concatenate([near_cand, candidates]), jnp.concatenate([candidates, near_cand]))
    table, median, here = reach_tables(tx_power.reshape(1, -1), site_position, held[0], half, depth, pixels, height)
    one = stage_one(cand, table, pieces, [here] + [held[k] for k in range(1, lines)], partner, half, depth)
    ends = [s for s in range(n) if s // lines in (0, 3)]
    inner = [s for s in range(n) if s // lines in (1, 2)]
    sums = [swap(one[0], 2 * lines, sources=ends), swap(one[0], 3 * lines, sources=ends)]
    own, hop = stage_two(cand, one, median, far, half, depth)
    moved = swap(hop, lines, sources=inner)
    best_level, sinr_level, share = finish(own, moved, sums, lines, bands)
    bit = 1
    while bit < bands:
        share = share + swap(share, bit, axis="band")
        bit *= 2
    return best_level, sinr_level, share[0, :1]


def solution(mesh):
    placed = (
        P("site", None, "band"),
        P("site", None, None),
        P("site", None),
        P(),
        P(),
        P("site", None),
    )

    return jax.shard_map(
        shards,
        mesh=mesh,
        in_specs=placed,
        out_specs=(P("site", "band"), P("site", "band"), P("site")),
        check_vma=False,
    )
```

```python
import functools
import math

import jax
import jax.numpy as jnp
from jax import lax
from jax.experimental import pallas as pl
from jax.experimental.pallas import tpu as pltpu
from jax.sharding import PartitionSpec as P


COLS = 256
spacing = 0.03
ln_tenth = 0.2302585093
to_exp2 = ln_tenth * math.log2(math.e)
dist_gain = to_exp2 * 11.0 * math.log10(2.0)
mixed_gain = to_exp2 * 8.0
F32 = jnp.float32
BF16 = jnp.bfloat16
SHARES = 2
HBM = pl.BlockSpec(memory_space=pltpu.HBM)
SMEM = pl.BlockSpec(memory_space=pltpu.SMEM)
VMEM = pl.BlockSpec(memory_space=pltpu.VMEM)


def places():
    return lax.axis_index("site"), lax.axis_index("band")


def grant(*parts):
    size = sum(math.prod(shape) * jnp.dtype(kind).itemsize for shape, kind in parts)
    return pltpu.CompilerParams(vmem_limit_bytes=min(size + (8 << 20), 60 << 20))


def split_tiles(fields, factor, pattern, lines):
    block, tiles, pixels = fields.shape
    depth = factor.shape[1]
    chunk = min(block, max(1, 256 // tiles))
    part = block // SHARES
    wide = depth * block

    steps = block // chunk

    def kernel(pattern_ref, x_ref, factor_ref, *refs):
        outs, (coef_out, x_in, factor_in, pattern_in, sems) = refs[: 3 * lines], refs[3 * lines :]
        me, band = places()
        copies = [pltpu.make_async_copy(factor_ref.at[pl.ds(band % SHARES * part, part)], factor_in, sems.at[steps])]
        for i in range(steps):
            span = slice(i * chunk, (i + 1) * chunk)
            copies.append(pltpu.make_async_copy(x_ref.at[span], x_in.at[span], sems.at[i]))
        copies.append(pltpu.make_async_copy(pattern_ref, pattern_in, sems.at[steps + 1]))
        for copy in copies:
            copy.start()
        size = chunk * tiles
        row = lax.broadcasted_iota(jnp.int32, (size, size), 0)
        col = lax.broadcasted_iota(jnp.int32, (size, size), 1)
        slot = row // chunk
        kind, k, j = slot // (2 * lines), slot // 2 % lines, slot % 2
        second = ((me // lines) & 1) ^ 1 ^ kind
        tile = jnp.where(second == 1, 3 - j, j) * lines + ((me % lines) ^ k)
        move = jnp.where(col == row % chunk * tiles + tile, 1.0, 0.0)
        copies[0].wait()
        copies[-1].wait()
        row = lax.broadcasted_iota(jnp.int32, (part, block), 0) + band % SHARES * part
        col = lax.broadcasted_iota(jnp.int32, (part, block), 1)
        rows = factor_in[...].astype(F32)
        for d in range(depth):
            keep = col <= row if d == 0 else jnp.full((part, block), pattern_in[0, d - 1], jnp.int32) != 0
            lane = (depth - 1 - d) * block
            coef_out[:, lane : lane + block] = jnp.where(keep, rows[:, d, :], 0.0).astype(BF16)
        for i in range(steps):
            copies[i + 1].wait()
            rows = slice(i * chunk, (i + 1) * chunk)
            for c in range(0, pixels, 256):
                span = slice(c, c + 256)
                x = x_in[rows, :, span].astype(F32).reshape(size, 256)
                moved = jnp.dot(move, x, preferred_element_type=F32).astype(BF16)
                for p in range(tiles):
                    unit = moved[p * chunk : (p + 1) * chunk]
                    if p < 2 * lines:
                        outs[p][rows, span] = unit
                    else:
                        outs[lines + p // 2][p % 2, rows, span] = unit

    shapes = [((block, pixels), BF16)] * (2 * lines) + [((2, block, pixels), BF16)] * lines + [((part, wide), BF16)]
    scratch = [((block, tiles, pixels), BF16), ((part, depth, block), BF16)]
    out = pl.pallas_call(
        kernel,
        in_specs=[HBM] * 3,
        out_specs=[VMEM] * (3 * lines + 1),
        out_shape=[jax.ShapeDtypeStruct(*shape) for shape in shapes],
        scratch_shapes=[pltpu.VMEM(*one) for one in scratch]
        + [pltpu.SMEM(pattern.shape, jnp.int32), pltpu.SemaphoreType.DMA((steps + 2,))],
        compiler_params=grant(*shapes, *scratch),
        name="split_tiles",
    )(*[pltpu.with_memory_space_constraint(x, pltpu.HBM) for x in (pattern, fields, factor)])
    first = [out[2 * k : 2 * k + 2] for k in range(lines)]
    return first, out[2 * lines : 3 * lines], out[-1]


def tile_of(me, lines, j):
    level = me // lines
    return jnp.where(level % 2 == 1, j, 3 - j) * lines + me % lines


def column(ref, row, i, block):
    line = ref[pl.ds(row, 1), pl.ds(pl.multiple_of(i * block, block), block)]
    return jnp.broadcast_to(line, (block, block)).T


def geometry(tx_ref, pos_ref, i, block, height):
    xs = column(pos_ref, 0, i, block) * (8.0 * COLS * spacing)
    ys = column(pos_ref, 1, i, block) * (height * COLS * spacing)
    base = to_exp2 * (column(tx_ref, 0, i, block) - 10.0)
    wide = COLS // block
    return jnp.concatenate([xs] * wide, axis=1), ys, jnp.concatenate([base] * wide, axis=1)


def across(xs, tile):
    col = lax.broadcasted_iota(jnp.int32, (1, COLS), 1)
    dx = xs - (tile % 8 * COLS + col).astype(F32) * spacing
    return dx * dx


def reach(dx2, ys, base, tile, row):
    at = jnp.full(ys.shape, tile // 8 * COLS + row, jnp.int32).astype(F32) * spacing
    dy = ys - at
    dy2 = dy * dy + spacing * spacing
    d2 = dx2 + jnp.concatenate([dy2] * (COLS // ys.shape[1]), axis=1)
    return base - dist_gain * jnp.log2(d2)


def rounded(mixed):
    return mixed_gain * mixed.astype(BF16).astype(F32)


def fold(power):
    return jnp.sum(power.reshape(power.shape[0] // 8, 8, power.shape[1]), axis=0)


def pick(cand_ref, j, first_site, pw, top, block):
    pixels = pw.shape[1]
    best = jnp.full((1, pixels), -1.0, F32)
    serving = jnp.zeros((1, pixels), jnp.int32)
    for c in range(cand_ref.shape[1]):
        local = jnp.clip(cand_ref[j, c] - first_site, 0, block - 1)
        power = pw[pl.ds(top + local, 1), :]
        more = power > best
        best = jnp.where(more, power, best)
        serving = jnp.where(more, local, serving)
    rest = []
    for c in range(0, pixels, COLS):
        ids = lax.broadcasted_iota(jnp.int32, (block, COLS), 0)
        mine = pw[pl.ds(top, block), c : c + COLS]
        rest.append(fold(jnp.where(ids == serving[:, c : c + COLS], 0.0, mine)))
    return best, jnp.concatenate(rest, axis=1)


def fill_table(out, tx_ref, pos_ref, place, i, half, height):
    me, band = places()
    block = tx_ref.shape[1] // (2 * half)
    pixels = out.shape[2]
    rows = pixels // COLS
    xs, ys, base = geometry(tx_ref, pos_ref, i, block, height)
    for j in range(2):
        tile = tile_of(me, half // 2, j)
        dx2 = across(xs, tile)
        for r in range(rows):
            span = slice(r * COLS, (r + 1) * COLS)
            out[j, pl.ds(place, block), span] = reach(dx2, ys, base, tile, band * rows + r)


def reach_tables(tx, pos, units, half, depth, pixels, height):
    block = tx.shape[1] // (2 * half)
    lead = depth - 1

    def kernel(tx_ref, pos_ref, unit0, unit1, table, out0, out1):
        out0[...] = unit0[...]
        out1[...] = unit1[...]
        me, _ = places()
        upper = me // half

        def body(l, carry):
            fill_table(table, tx_ref, pos_ref, pl.multiple_of(l * block, block), upper * half + l, half, height)
            return carry

        lax.fori_loop(upper * lead, half, body, 0)

    outs = [((2, half * block, pixels), F32)] + [(unit.shape, BF16) for unit in units]
    flops = 20 * 2 * half * block * pixels
    return pl.pallas_call(
        kernel,
        in_specs=[VMEM] * 4,
        out_specs=[VMEM] * 3,
        out_shape=[jax.ShapeDtypeStruct(*out) for out in outs],
        compiler_params=grant(*outs, *outs[1:]),
        cost_estimate=pl.CostEstimate(flops=flops, bytes_accessed=8 << 20, transcendentals=0),
        name="reach_tables",
    )(tx, pos, *units)


def middle_tables(tx, pos, half, depth, pixels, height):
    block = tx.shape[1] // (2 * half)
    lead, lines = depth - 1, half // 2

    def kernel(tx_ref, pos_ref, median):
        me, _ = places()
        level = me // lines

        @pl.when((level == 1) | (level == 2))
        def _():
            def body(l, carry):
                fill_table(median, tx_ref, pos_ref, pl.multiple_of(l * block, block), half + l, half, height)
                return carry

            lax.fori_loop(0, lead, body, 0)

    out = ((2, lead * block, pixels), F32)
    flops = 20 * 2 * lead * block * pixels
    return pl.pallas_call(
        kernel,
        in_specs=[VMEM] * 2,
        out_specs=VMEM,
        out_shape=jax.ShapeDtypeStruct(*out),
        compiler_params=grant(out),
        cost_estimate=pl.CostEstimate(flops=flops, bytes_accessed=4 << 20, transcendentals=0),
        name="middle_tables",
    )(tx, pos)


def stage_one(at_ends, cand, table, pieces, ends_rows, held, partner, half, depth):
    block, pixels = held[0].shape
    lead, lines = depth - 1, half // 2
    rows = pixels // COLS
    n, part, wide = 2 * half, pieces[0].shape[2], depth * block
    np_, nh = len(pieces), len(partner)
    tall = lead * block

    def kernel(cand_ref, table_ref, *refs):
        piece_refs, refs = refs[:np_], refs[np_:]
        held_refs, refs = refs[: 2 * nh], refs[2 * nh :]
        partner_refs, refs = refs[:nh], refs[nh:]
        if at_ends:
            sums, near, coef, coef_own, group, pw, acc = refs
        else:
            sums, best_out, partial, coef_cross, near, coef, coef_own, group, pw, acc = refs
        me, band = places()
        upper = me // half
        low = upper * half
        level = me // lines
        inner = (level == 1) | (level == 2)
        active = jnp.logical_not(inner) if at_ends else inner

        @pl.when(active)
        def _():
            for m, piece in enumerate(piece_refs):
                there = pl.ds(pl.multiple_of((band % SHARES ^ m) * part, part), part)
                for i, high in enumerate(ends_rows):
                    coef[3 * lines + high, there, :] = piece[3 + i, 0]
                for k in range(lines):
                    coef[me ^ 3 * lines ^ k, there, :] = piece[2, k]
                for k in range(lines):
                    coef[me ^ lines ^ k, there, :] = piece[1, k]
                    coef[me ^ k, there, :] = piece[0, k]
            near[:, :lead] = jnp.zeros((2, lead, block, pixels), BF16)
            for k in range(lines):
                for j in range(2):
                    near[j, lead + (me ^ k) - low] = held_refs[2 * k + j][...]
                    near[j, lead + (me ^ k ^ lines) - low] = partner_refs[k][j]
            acc[...] = jnp.zeros_like(acc)
            if not at_ends:
                best_out[...] = jnp.zeros_like(best_out)
                up = jnp.full((block, block), upper, jnp.int32) != 0
                for l in range(lead):
                    for c in range(lead):
                        zero = jnp.zeros((block, block), BF16)
                        early = coef[half + l, :, (c - l) * block : (c - l + 1) * block] if c >= l else zero
                        at = lead - l + c
                        late = coef[half + l, :, at * block : (at + 1) * block] if c <= l else zero
                        there = (slice(l * block, (l + 1) * block), slice(c * block, (c + 1) * block))
                        early, late = early.astype(F32), late.astype(F32)
                        coef_own[there] = jnp.where(up, late, early).astype(BF16)
                        coef_cross[there] = jnp.where(up, early, late).astype(BF16)
                top = jnp.where(upper == 0, half, lead)
                for j in range(2):
                    for r in range(rows):
                        span = slice(r * COLS, (r + 1) * COLS)
                        some = near[j, pl.ds(top, lead), :, span].reshape(tall, COLS)
                        partial[j, :, span] = jnp.dot(coef_own[...], some, preferred_element_type=F32)

            first = upper * lead

            def add(j, i, span, power):
                if at_ends:
                    acc[j, :, span] += fold(power)
                    return
                own = i == tile_of(me, lines, j)

                @pl.when(own)
                def _():
                    pw[j, :, span] = power

                acc[j, :, span] += jnp.where(own, 0.0, fold(power))

            @pl.when(upper == 0)
            def _():
                for g in range(0, half, depth):
                    count = min(depth, half - g)
                    start = max(0, g - lead)
                    deep = g + count - start
                    for a in range(count):
                        for b in range(deep):
                            d = g + a - start - b
                            there = (slice(a * block, (a + 1) * block), slice(b * block, (b + 1) * block))
                            if 0 <= d < depth:
                                group[there] = coef[g + a, :, (lead - d) * block : (depth - d) * block]
                            else:
                                group[there] = jnp.zeros((block, block), BF16)
                    for j in range(2):
                        for r in range(rows):
                            span = slice(r * COLS, (r + 1) * COLS)
                            some = near[j, lead + start : lead + start + deep, :, span].reshape(deep * block, COLS)
                            here = slice(g * block, (g + count) * block)
                            mixed = jnp.dot(group[: count * block, : deep * block], some, preferred_element_type=F32)
                            power = jnp.exp2(table_ref[j, here, span] + rounded(mixed))
                            for a in range(count):
                                add(j, g + a, span, power[a * block : (a + 1) * block])

            @pl.when(upper != 0)
            def _():
                def body(l, carry):
                    for j in range(2):
                        for r in range(rows):
                            span = slice(r * COLS, (r + 1) * COLS)
                            some = near[j, pl.ds(l, depth), :, span].reshape(depth * block, COLS)
                            mixed = rounded(jnp.dot(coef[half + l], some, preferred_element_type=F32))
                            here = pl.ds(pl.multiple_of(l * block, block), block)
                            add(j, half + l, span, jnp.exp2(table_ref[j, here, span] + mixed))
                    return carry

                lax.fori_loop(lead, half, body, 0)

            for j in range(2):
                tile = tile_of(me, lines, j)

                @pl.when(jnp.logical_not(at_ends) & (tile >= low + first) & (tile < low + half))
                def _():
                    if at_ends:
                        return
                    best, rest = pick(cand_ref, j, tile * block, pw.at[j], 0, block)
                    best_out[j : j + 1] = best
                    acc[j] += rest

                sums[j : j + 1] = jnp.sum(acc[j], axis=0, keepdims=True)

    flops = (half * 2 + lead) * 2 * block * depth * block * pixels
    scratch = [
        ((2, lead + half, block, pixels), BF16),
        ((n, block, wide), BF16),
        ((tall, tall), BF16),
        ((depth * block, (depth + lead) * block), BF16),
        ((2, block, pixels), F32),
        ((2, 8, pixels), F32),
    ]
    outs = [((2, pixels), F32)]
    if not at_ends:
        outs += [((2, pixels), F32), ((2, tall, pixels), F32), ((tall, tall), BF16)]
    given = (table, *pieces, *held, *partner)
    return pl.pallas_call(
        kernel,
        in_specs=[SMEM] + [VMEM] * len(given),
        out_specs=[VMEM] * len(outs),
        out_shape=[jax.ShapeDtypeStruct(*out) for out in outs],
        scratch_shapes=[pltpu.VMEM(*one) for one in scratch],
        compiler_params=grant(*scratch, *outs, *[(x.shape, x.dtype) for x in given]),
        cost_estimate=pl.CostEstimate(flops=flops, bytes_accessed=8 << 20, transcendentals=0),
        name="stage_one",
    )(cand, *given)


def stage_two(cand, one, median, other, middle, outer, half, depth, bands):
    block, pixels = one[2].shape[1] // (depth - 1), one[2].shape[2]
    lead, lines = depth - 1, half // 2
    rows = pixels // COLS
    tall = lead * block
    nm, no = len(middle), len(outer)

    def kernel(cand_ref, sums, best_one, partial, coef, median, other_ref, *refs):
        middle_refs, refs = refs[:nm], refs[nm:]
        outer_refs, refs = refs[: 2 * no], refs[2 * no :]
        outs, (far, pw, acc, best) = refs[:2], refs[2:]
        me, _ = places()
        upper = me // half
        level = me // lines

        @pl.when((level == 1) | (level == 2))
        def _():
            base = jnp.where(upper == 0, half, half - lead)

            def put(j, row, unit):
                place = row - base
                far[j, jnp.where((place >= 0) & (place < lead), place, lead)] = unit

            for j in range(2):
                for (k, _), ref in zip(middle, middle_refs):
                    put(j, me ^ 3 * lines ^ k, ref[j])
                for i, (low, high, _) in enumerate(outer):
                    put(j, jnp.where(upper == 0, 3 * lines + high, low), outer_refs[2 * i + j][...])
                best[...] = best_one[j : j + 1]
                tile = tile_of(me, lines, j)
                for r in range(rows):
                    span = slice(r * COLS, (r + 1) * COLS)
                    some = far[j, :lead, :, span].reshape(tall, COLS)
                    mixed = jnp.dot(coef[...], some, preferred_element_type=F32) + partial[j, :, span]
                    power = jnp.exp2(median[j, :, span] + rounded(mixed))
                    total = jnp.zeros((8, COLS), F32)
                    for l in range(lead):
                        total += jnp.where(tile == half + l, 0.0, fold(power[l * block : (l + 1) * block]))
                    acc[:, span] = total

                    @pl.when(upper != 0)
                    def _():
                        pw[:, span] = power

                @pl.when((tile >= half) & (tile < half + lead))
                def _():
                    top = pl.multiple_of((tile - half) * block, block)
                    first, rest = pick(cand_ref, j, tile * block, pw, top, block)
                    best[...] = first
                    acc[...] += rest

                total = sums[j : j + 1] + other_ref[j : j + 1] + jnp.sum(acc[...], axis=0, keepdims=True)
                scale = 1.0 / math.log(10.0)
                sinr = jnp.log(best[...] / total) * scale
                share = jnp.sum(sinr, axis=1, keepdims=True) / float(pixels * bands)
                outs[j][0:1] = jnp.log(best[...]) * scale
                outs[j][1:2] = sinr
                outs[j][2:3] = jnp.broadcast_to(share, (1, pixels))

    scratch = [((2, lead + 1, block, pixels), BF16), ((tall, pixels), F32), ((8, pixels), F32), ((1, pixels), F32)]
    given = [x for _, x in middle] + [x for _, _, pair in outer for x in pair]
    held = [(x.shape, x.dtype) for x in (*one[2:], median, *given)]
    return pl.pallas_call(
        kernel,
        in_specs=[SMEM] + [VMEM] * (6 + len(given)),
        out_specs=[VMEM] * 2,
        out_shape=[jax.ShapeDtypeStruct((3, pixels), F32)] * 2,
        scratch_shapes=[pltpu.VMEM(*shape) for shape in scratch],
        compiler_params=grant(*scratch, *held),
        name="stage_two",
    )(cand, *one, median, other, *given)


def plan_of(n, lead):
    half, lines = n // 2, n // 4
    cross = range(half - lead, half + lead)
    row = lambda s, k: s // lines * lines + (s % lines ^ k)
    middle = {k: [s for s in range(n) if s // lines in (1, 2) and row(s, k) in cross] for k in range(lines)}
    low = [r for r in range(lines) if r in cross]
    high = [r for r in range(lines) if 3 * lines + r in cross]
    assert len(low) == len(high)
    return middle, list(zip(low, high))


def shards(fields, factor, pattern, tx_power, site_position, candidates):
    _, tiles, pixels = fields.shape
    depth = factor.shape[1]
    n, bands = lax.axis_size("site"), lax.axis_size("band")
    half, lines, lead = n // 2, n // 4, depth - 1
    assert tiles == n and half >= lead
    height = tiles // 8
    middle, outer = plan_of(n, lead)
    me = lax.axis_index("site")
    level = me // lines

    def swap(x, k, axis="site", sources=None):
        count = n if axis == "site" else bands
        sources = range(count) if sources is None else sources
        return lax.ppermute(x, axis, [(s, s ^ k) for s in sources])

    class0, class1, own_part = split_tiles(fields, factor, pattern, lines)

    ends = [s for s in range(n) if s // lines in (0, 3)]
    pass_on = {0: class1[0]}
    pass_on.update({k: swap(class1[k], k) for k in range(1, lines)})
    held = {0: class0[0]}
    held.update({k: [swap(class0[k][j], k) for j in range(2)] for k in range(1, lines)})
    far = [(k, swap(pass_on[k], 3 * lines, sources=middle[k])) for k in range(lines) if middle[k]]
    partner = [swap(pass_on[k], lines) for k in range(lines)]
    ends_far = []
    for low, high in outer:
        at = (me % lines) ^ jnp.where(level == 0, low, high)
        pair = []
        for j in range(2):
            here, _ = lax.optimization_barrier((at, jnp.int32(j)))
            unit = held[0][j]
            for k in range(1, lines):
                unit = jnp.where(here == k, held[k][j], unit)
            pair.append(swap(unit, 2 * lines, sources=ends))
        ends_far.append((low, high, pair))

    line_part = jnp.stack([own_part] + [swap(own_part, k) for k in range(1, lines)])
    next_part = swap(line_part, lines)
    middle_part = swap(line_part, 3 * lines, sources=range(2 * lines, 3 * lines))
    ends_part = []
    for low, high in outer:
        at = (me % lines) ^ high
        row = line_part[0]
        for k in range(1, lines):
            row = jnp.where(at == k, line_part[k], row)
        ends_part.append(swap(row, 2 * lines, sources=range(3 * lines, n)))
    groups = [line_part, next_part, middle_part] + [jnp.broadcast_to(x[None], line_part.shape) for x in ends_part]
    mine = jnp.stack(groups)
    pieces = [mine, swap(mine, 1, axis="band")]

    near_cand = swap(candidates, lines)
    cand = jnp.concatenate([near_cand, candidates])
    tx = tx_power.reshape(1, -1)
    table, *here = reach_tables(tx, site_position, held[0], half, depth, pixels, height)
    median = middle_tables(tx, site_position, half, depth, pixels, height)
    units = here + [x for k in range(1, lines) for x in held[k]]
    stage = functools.partial(
        stage_one,
        table=table,
        pieces=pieces,
        ends_rows=[high for _, high in outer],
        held=units,
        partner=partner,
        half=half,
        depth=depth,
    )
    (ends_sums,) = stage(True, cand)
    other = swap(ends_sums, 2 * lines, sources=ends)
    one = stage(False, cand)
    inner = [s for s in range(n) if s // lines in (1, 2)]
    moving, own = stage_two(cand, one, median, other, far, ends_far, half, depth, bands)
    moved = swap(moving, lines, sources=inner)
    done = jnp.where((level == 1) | (level == 2), own, moved)
    share = done[2:3, :128]
    bit = 1
    while bit < bands:
        share = share + swap(share, bit, axis="band")
        bit *= 2
    return done[0:1], done[1:2], share[0, :1]


def solution(mesh):
    placed = (
        P("site", None, "band"),
        P("site", None, None),
        P("site", None),
        P(),
        P(),
        P("site", None),
    )

    return jax.shard_map(
        shards,
        mesh=mesh,
        in_specs=placed,
        out_specs=(P("site", "band"), P("site", "band"), P("site")),
        check_vma=False,
    )
```
